32 devices in a mesh: inst: 2 (over x), panel: 8 (over z, y), obs: 2 (over core).
Axes of the slice: x: 2, y: 2, z: 4, core: 2. Of those that a mesh axis runs over, the one named last changes fastest.
Arguments:
- sources: bfloat16 [8, 4, 2048], P('inst', None, ('panel', 'obs')), may hold values from -12 to 12
- panel_positions: float32 [3, 2048], P(None, ('panel', 'obs')), may hold values from -1 to 1
- panel_copy: int32 [2048], P(('panel', 'obs')), may hold values from 0 to 2
- harmonic_numbers: int32 [3], replicated, may hold values from 1 to 3
- blade_count: int32 [1], replicated, may hold values from 3 to 34
- observer_ids: int32 [2, 128, 128], P('obs'), may hold values from 0 to 131071
- observer_radius: float32 [2, 128, 128], P('obs'), may hold values from 4 to 12
Outputs:
- pressure: float32 [2, 128, 2, 3, 128], P('obs', ('inst', 'panel'))
The draws below stay inside these ranges and needn't reach their ends.
Inputs may be any that keep to these rules, and one draw needn't show every extreme that they name: `harmonic_numbers`: each is a harmonic number below 4. `panel_copy`: always below blade_count. `observer_ids`: an index on a grid of 256 polar by 512 azimuthal angles, not necessarily distinct.
All inputs are finite; a program needn't handle non-finite values.
Results may differ from the reference program's by a relative error of at most 0.0003.
Values may be sent and summed in bfloat16 or wider, within the bound.
No kernel may reach another device: no remote copies, remote signals or barrier semaphores. Data moves between devices by JAX's collectives and lax.ppermute only.
A program may use at most 64 MiB of HBM per device.

```python
import math
import jax
import jax.numpy as jnp
from jax import lax

INSTANCES = 8
HARM = 3
COMP = 4
PANELS = 2048
LANE = 128
LISTENER_SETS = 128
OBS_GROUPS = 2
NTHETA = 256
NPHI = 512


def plant(entries, key, smallest, largest):
    index_at = [jax.random.randint(jax.random.fold_in(key, axis), (), 0, length) for axis, length in enumerate(entries.shape)]
    main_axis = entries.shape.index(max(entries.shape))
    neighbour = index_at[:main_axis] + [(index_at[main_axis] + 1) % entries.shape[main_axis]] + index_at[main_axis + 1:]
    return entries.at[tuple(index_at)].set(smallest).at[tuple(neighbour)].set(largest)


def steps_of(key, dims, pieces, least, top_value):
    loudness, own = 1.0, jax.random.fold_in(key, 6)
    for dim, blocks in pieces:
        draws = jnp.exp(jax.random.uniform(jax.random.fold_in(own, dim), (blocks,), jnp.float32, least / len(pieces), top_value / len(pieces)))
        loudness = loudness * jnp.repeat(draws, dims[dim] // blocks).reshape([-1 if axis == dim else 1 for axis in range(len(dims))])
    return loudness


def noise(own_key, extent, deviation, most, cuts=(), held_as=jnp.bfloat16):
    array = jax.random.normal(own_key, extent, jnp.float32) * deviation
    if len(cuts) > 0:
        array = steps_of(own_key, extent, cuts, -0.22, 0.18) * array
    return jnp.clip(array, min=-most, max=most).astype(held_as)


def setup_inputs(seed: int = 0) -> dict:
    keys = jax.random.split(jax.random.key(seed), 8)
    return {
        "sources": noise(keys[0], (INSTANCES, COMP, PANELS), 2.0, 12.0, ((0, 2), (2, 16))),
        "panel_positions": jnp.clip(jax.random.uniform(keys[1], (3, PANELS), jnp.float32, -1.0, 1.0) * steps_of(keys[1], (3, PANELS), ((1, 16),), -0.4, 0.0), -1.0, 1.0),
        "panel_copy": plant(jax.random.randint(keys[2], (PANELS,), 0, 3), jax.random.fold_in(keys[2], 1), 0, 2).astype(jnp.int32),
        "harmonic_numbers": jax.random.randint(keys[3], (HARM,), 1, INSTANCES // 2).astype(jnp.int32),
        "blade_count": jax.random.randint(keys[4], (1,), 3, 35).astype(jnp.int32),
        "observer_ids": plant(jax.random.randint(keys[5], (OBS_GROUPS, LISTENER_SETS, LANE), 0, NTHETA * NPHI), jax.random.fold_in(keys[5], 1), 0, (NTHETA * NPHI) - 1).astype(jnp.int32),
        "observer_radius": jnp.clip(jnp.exp(math.log(12.0) - 1.0986123 * jax.random.uniform(keys[6], (OBS_GROUPS, LISTENER_SETS, LANE), jnp.float32) ** steps_of(keys[6], (OBS_GROUPS, LISTENER_SETS, LANE), ((0, 2),), -0.2, 0.2)), 4.0, 12.0),
    }


WAVE_UNIT = 0.05
QUADRUPLE_CIRCLE = 4.0 * 3.141592653589793
TWO_PI = 2.0 * 3.141592653589793

def dft_table(multiple_indices, starting_snapshot, per_chip_sample_sum, snapshot_number):
    sample_moments = starting_snapshot + jnp.arange(per_chip_sample_sum, dtype=jnp.int32)
    rotation_angles_list = multiple_indices[:, None] * sample_moments[None, :] % snapshot_number
    angles = TWO_PI * rotation_angles_list.astype(jnp.float32) / snapshot_number
    return jnp.concatenate([jnp.cos(angles), -jnp.sin(angles)], axis=0) / snapshot_number

def rotate_panels(spectra, panel_xyz, panel_copy, blade_count):
    angles = TWO_PI * panel_copy.astype(jnp.float32) / blade_count[0].astype(jnp.float32)
    cosine = jnp.cos(angles)
    sine_part = jnp.sin(angles)
    moved_xyz = jnp.stack([cosine * panel_xyz[0] - sine_part * panel_xyz[1], sine_part * panel_xyz[0] + cosine * panel_xyz[1], panel_xyz[2]])
    along_x = spectra[:, :, 1]
    along_y = spectra[:, :, 2]
    moved = jnp.stack([spectra[:, :, 0], cosine * along_x - sine_part * along_y, sine_part * along_x + cosine * along_y, spectra[:, :, 3]], axis=2)
    return (moved, moved_xyz)

def observer_coords(observer_ids, observer_radius):
    polar_index = observer_ids // NPHI
    azimuth_index = observer_ids % NPHI
    theta = 3.141592653589793 * (polar_index.astype(jnp.float32) + 0.5) / NTHETA
    azimuth = TWO_PI * azimuth_index.astype(jnp.float32) / NPHI
    sine_theta = jnp.sin(theta)
    return (observer_radius * sine_theta * jnp.cos(azimuth), observer_radius * sine_theta * jnp.sin(azimuth), observer_radius * jnp.cos(theta))

def panel_term(coords, wavenumbers, spectrum, source_xyz):
    delta_x = coords[0] - source_xyz[0]
    delta_y = coords[1] - source_xyz[1]
    delta_z = coords[2] - source_xyz[2]
    distance = jnp.sqrt(delta_x * delta_x + delta_y * delta_y + delta_z * delta_z)
    inverse = 1.0 / distance
    spread = inverse / QUADRUPLE_CIRCLE
    near_field = spread * inverse * inverse
    real_parts = []
    imag_parts = []
    for number in range(wavenumbers.shape[0]):
        wavenumber = wavenumbers[number]
        phase_arg = wavenumber * distance
        cosine = jnp.cos(phase_arg)
        sine_part = jnp.sin(phase_arg)
        mono_real = spectrum[0, number, 0]
        mono_imag = spectrum[1, number, 0]
        dipole_real = spectrum[0, number, 1] * delta_x + spectrum[0, number, 2] * delta_y + spectrum[0, number, 3] * delta_z
        dipole_imag = spectrum[1, number, 1] * delta_x + spectrum[1, number, 2] * delta_y + spectrum[1, number, 3] * delta_z
        factor_real = cosine + phase_arg * sine_part
        factor_imag = phase_arg * cosine - sine_part
        real_parts.append(wavenumber * spread * (mono_real * sine_part - mono_imag * cosine) + near_field * (dipole_real * factor_real - dipole_imag * factor_imag))
        imag_parts.append(wavenumber * spread * (mono_real * cosine + mono_imag * sine_part) + near_field * (dipole_real * factor_imag + dipole_imag * factor_real))
    return (real_parts, imag_parts)

def reference(sources, panel_positions, panel_copy, harmonic_numbers, blade_count, observer_ids, observer_radius):
    snapshot_number = sources.shape[0]
    dft_rows = dft_table(harmonic_numbers, 0, snapshot_number, snapshot_number)
    spectra = jnp.einsum('hn,ncp->hcp', dft_rows, sources.astype(jnp.float32), precision=lax.Precision.HIGHEST)
    spectra = spectra.reshape(2, HARM, COMP, PANELS)
    spectra, panel_xyz = rotate_panels(spectra, panel_positions, panel_copy, blade_count)
    coords = observer_coords(observer_ids, observer_radius)
    flat_coords = tuple((member.reshape(-1, 1) for member in coords))
    wavenumbers = harmonic_numbers.astype(jnp.float32) * blade_count[0].astype(jnp.float32) * WAVE_UNIT
    tile_size = 16
    tile_count = PANELS // tile_size
    spectrum_tiles = jnp.moveaxis(spectra.reshape(2, HARM, COMP, tile_count, tile_size), 3, 0)
    xyz_tiles = jnp.moveaxis(panel_xyz.reshape(3, tile_count, tile_size), 1, 0)

    def advance(current, record):
        spectrum, source_xyz = record
        real_parts, imag_parts = panel_term(flat_coords, wavenumbers, spectrum, source_xyz)
        return (tuple((running + lax.optimization_barrier(jnp.sum(addend, axis=1)) for running, addend in zip(current, real_parts + imag_parts))), None)
    empty_sums = tuple((jnp.zeros((flat_coords[0].shape[0],), jnp.float32) for number in range(2 * HARM)))
    totals, unused = lax.scan(advance, empty_sums, (spectrum_tiles, xyz_tiles))
    totals = tuple((member.reshape(observer_ids.shape) for member in totals))
    stacked = jnp.stack([jnp.stack(totals[:HARM]), jnp.stack(totals[HARM:])])
    return jnp.transpose(stacked, (2, 3, 0, 1, 4))
```

```python
import functools
import math

import jax
import jax.numpy as jnp
import numpy as np
from jax import lax
from jax.experimental import pallas as pl
from jax.experimental.pallas import tpu as pltpu
from jax.sharding import PartitionSpec as P

NTHETA = 256
NPHI = 512
WAVE_UNIT = 0.05
TWO_PI = 2.0 * 3.141592653589793
LANES = 128
TILE = 256
CHUNK = 256
HELD_TILES = 8
FEATURES = 8
PARTS = 6
DEPTH = FEATURES * PARTS

HALF_SINE = (6.28317247, -10.33464405, 5.08745911, -1.11966943)


def split_parts(value):
    high = value.astype(jnp.bfloat16).astype(jnp.float32)
    rest = value - high
    middle = rest.astype(jnp.bfloat16).astype(jnp.float32)
    return high, middle, rest - middle


def pack_kernel(blades_ref, src_ref, pos_ref, copy_ref, out_ref):
    inst_here = lax.axis_index("inst")
    angle = TWO_PI * copy_ref[...].astype(jnp.float32) / blades_ref[0].astype(jnp.float32)
    cosine, sine = jnp.cos(angle), jnp.sin(angle)
    x, y, z = pos_ref[0:1, :], pos_ref[1:2, :], pos_ref[2:3, :]
    values = (cosine * x - sine * y, sine * x + cosine * y, z, cosine, sine)
    parts = [split_parts(value) for value in values]
    rows = [parts[i][j] for j in range(3) for i in range(5)]
    rows.append(jnp.zeros_like(z))
    own = jnp.where(inst_here == 0, jnp.concatenate(rows[:8], axis=0), jnp.concatenate(rows[8:], axis=0))
    terms = [src_ref[n].astype(jnp.float32) for n in range(src_ref.shape[0])]
    block = jnp.concatenate(terms + [own], axis=0).astype(jnp.bfloat16)

    def put(d, carry):
        out_ref[d] = block
        return carry

    lax.fori_loop(0, out_ref.shape[0], put, 0)


def pair_factors(t2, t0, orders):
    w = lax.rsqrt(t2)
    w3 = w * (1.0 / t2)
    t = t2 * w
    f = t - t0
    z = f * f
    s = jnp.float32(HALF_SINE[-1])
    for c in HALF_SINE[-2::-1]:
        s = s * z + jnp.float32(c)
    s = s * f
    q = s * s
    twice = 2.0 - q
    d = 4.0 - q
    cosine = w3 * twice
    sine = w3 * (s * (d * lax.rsqrt(d)))
    factors = {1: (cosine, sine)}
    if orders[-1] > 1:
        factors[2] = (twice * cosine - (w3 + w3), twice * sine)
    for m in range(3, orders[-1] + 1):
        (c1, s1), (c0, s0) = factors[m - 1], factors[m - 2]
        factors[m] = (twice * c1 - c0, twice * s1 - s0)
    return t, factors


def main_kernel(
    harm_ref, blades_ref, table_ref, got_ref, ids_ref, radius_ref, out_ref,
    feat_ref, hub_ref, coef_ref, acc_ref, rows_ref, *, insts, per_inst, comps, orders,
):
    block_rows = out_ref.shape[2]
    observers = block_rows * LANES
    groups = got_ref.shape[0] // insts
    tiles = groups * LANES // TILE
    held = min(HELD_TILES, tiles)
    per_tile = TILE // LANES
    src_rows = per_inst * comps
    count = len(orders)
    first = (lax.axis_index("inst") * lax.axis_size("panel") + lax.axis_index("panel")) * block_rows
    first = pl.multiple_of(first, 8)

    kappa = blades_ref[0].astype(jnp.float32) * WAVE_UNIT
    scale = kappa / TWO_PI

    ids = ids_ref[0, pl.ds(first, block_rows), :]
    radius = radius_ref[0, pl.ds(first, block_rows), :]
    theta = 3.141592653589793 * ((ids // NPHI).astype(jnp.float32) + 0.5) / NTHETA
    phi = TWO_PI * (ids % NPHI).astype(jnp.float32) / NPHI
    sine_theta = jnp.sin(theta)
    x1 = radius * sine_theta * jnp.cos(phi)
    x2 = radius * sine_theta * jnp.sin(phi)
    x3 = radius * jnp.cos(theta)
    hub = scale * radius
    features = (x1, x2, x3, jnp.ones_like(x1), radius * radius)
    for b in range(0, block_rows, 8):
        for i in range(FEATURES):
            value = features[i][b : b + 8] if i < len(features) else jnp.zeros((8, LANES), jnp.float32)
            rows_ref[i * 8 : (i + 1) * 8, :] = value
        for r in range(8):
            b1, b2, b3 = split_parts(rows_ref[pl.ds(r, FEATURES, stride=8), :])
            stack = [b1, b2, b3, b1, b2, b1, jnp.broadcast_to(hub[b + r : b + r + 1], (8, LANES))]
            stack.append(jnp.zeros((LANES - 8 * len(stack), LANES), jnp.float32))
            turned = jnp.concatenate(stack, axis=0).T
            at = slice((b + r) * LANES, (b + r + 1) * LANES)
            feat_ref[at, :] = turned[:, 0:DEPTH].astype(jnp.bfloat16)
            hub_ref[at, :] = jnp.broadcast_to(turned[:, DEPTH : DEPTH + 1], (LANES, LANES))

    row = lax.broadcasted_iota(jnp.int32, (8, TILE), 0)
    order_of_row = (row // 2 + 1).astype(jnp.float32)
    s2 = scale * scale
    s3 = s2 * scale
    far = s3 / (8.0 * 3.141592653589793)
    near = order_of_row * (s3 * 0.25)
    mono = order_of_row * (s2 * 0.25)

    def coefficients(first_tile):
        def one(j, carry):
            at = (first_tile + j) * per_tile
            src = [
                jnp.concatenate([got_ref[i * groups + at + p, 0:src_rows, :] for p in range(per_tile)], axis=1)
                for i in range(insts)
            ]
            src = jnp.concatenate(src, axis=0)
            spec = None
            for part in range(3):
                term = jnp.dot(table_ref[part], src, preferred_element_type=jnp.float32)
                spec = term if spec is None else spec + term
            turned_q, f1, f2, f3 = (spec[8 * c : 8 * c + 8] for c in range(4))
            geo = [
                jnp.concatenate(
                    [got_ref[i * groups + at + p, src_rows : src_rows + 8, :].astype(jnp.float32) for p in range(per_tile)],
                    axis=1,
                )
                for i in range(2)
            ]
            geo = [geo[i][r : r + 1] for i in range(2) for r in range(8)]
            y1, y2, y3, cosine, sine = (geo[i] + geo[5 + i] + geo[10 + i] for i in range(5))
            g1 = cosine * f1 - sine * f2
            g2 = sine * f1 + cosine * f2
            dipole = (g1, g2, f3, -(g1 * y1 + g2 * y2 + f3 * y3))
            square = y1 * y1 + y2 * y2 + y3 * y3
            distance = (-2.0 * s2 * y1, -2.0 * s2 * y2, -2.0 * s2 * y3, s2 * square, jnp.full_like(y1, s2))
            lifted = mono * turned_q
            zero = jnp.zeros((8, TILE), jnp.float32)

            def write(o, value):
                a1, a2, a3 = split_parts(value)
                coef_ref[o, j, 0:16, :] = jnp.concatenate([a1, a1], axis=0).astype(jnp.bfloat16)
                coef_ref[o, j, 16:32, :] = jnp.concatenate([a1, a2], axis=0).astype(jnp.bfloat16)
                coef_ref[o, j, 32:48, :] = jnp.concatenate([a2, a3], axis=0).astype(jnp.bfloat16)

            def keep(i, value):
                for p in range(per_tile):
                    rows_ref[(p * FEATURES + i) * 8 : (p * FEATURES + i + 1) * 8, :] = value[:, p * LANES : (p + 1) * LANES]

            def gathered(r):
                return jnp.concatenate(
                    [rows_ref[pl.ds(p * FEATURES * 8 + r, FEATURES, stride=8), :] for p in range(per_tile)], axis=1
                )

            write(0, jnp.concatenate(list(distance) + [zero[0:3]], axis=0))
            for i in range(FEATURES):
                value = zero
                if i < 4:
                    value = far * dipole[i] + lifted * distance[i]
                elif i == 4:
                    value = lifted * distance[i]
                keep(i, value)
            for m in range(3):
                for part in range(2):
                    write(1 + 4 * m + part, gathered(2 * m + part))
            for i in range(FEATURES):
                keep(i, near * dipole[i] if i < 4 else zero)
            for m in range(3):
                for part in range(2):
                    write(3 + 4 * m + part, gathered(2 * m + part))
            return carry

        lax.fori_loop(0, held, one, 0)

    def pair_sums(chosen):
        def step(it, carry):
            at = pl.multiple_of(it // held * CHUNK, CHUNK)
            j = it % held
            feat = feat_ref[pl.ds(at, CHUNK), :]

            def pair(o):
                return jnp.dot(feat, coef_ref[o, j], preferred_element_type=jnp.float32)

            squares = pair(0)
            pairs = {m: [pair(4 * m - 3 + i) for i in range(4)] for m in chosen}
            for v in range(CHUNK // 8):
                obs_rows = pl.ds(pl.multiple_of(at + v * 8, 8), 8)
                t0 = hub_ref[obs_rows, :]
                sums = {}
                for lane in range(TILE // LANES):
                    where = (slice(v * 8, v * 8 + 8), slice(lane * LANES, (lane + 1) * LANES))
                    t, factors = pair_factors(squares[where], t0, chosen)
                    for m in chosen:
                        cosine, sine = factors[m]
                        p_re, p_im, m_re, m_im = (matrix[where] for matrix in pairs[m])
                        real = p_re - t * m_im
                        imag = p_im + t * m_re
                        new = (cosine * real + sine * imag, cosine * imag - sine * real)
                        old = sums.get(m)
                        sums[m] = new if old is None else (old[0] + new[0], old[1] + new[1])
                for m in chosen:
                    for part in range(2):
                        o = 2 * (m - 1) + part
                        acc_ref[o, obs_rows, :] = acc_ref[o, obs_rows, :] + sums[m][part]
            return carry

        lax.fori_loop(0, observers // CHUNK * held, step, 0)

    acc_ref[...] = jnp.zeros_like(acc_ref)

    def chunk(i, carry):
        coefficients(i * held)
        pair_sums(orders)
        return carry

    lax.fori_loop(0, tiles // held, chunk, 0)

    turn = hub - jnp.round(hub)
    base = (jnp.cos(TWO_PI * turn), jnp.sin(TWO_PI * turn))
    lane_of = lax.broadcasted_iota(jnp.int32, (LANES, LANES), 1)
    collected = []
    for b in range(block_rows):
        matrix = jnp.zeros((LANES, LANES), jnp.float32)
        for o in range(2 * count):
            total = jnp.sum(acc_ref[o, b * LANES : (b + 1) * LANES, :], axis=1, keepdims=True)
            matrix = jnp.where(lane_of == o, total, matrix)
        collected.append(matrix.T[0:8])
    results = []
    phase = (jnp.ones_like(turn), jnp.zeros_like(turn))
    for m in range(count):
        phase = (phase[0] * base[0] - phase[1] * base[1], phase[0] * base[1] + phase[1] * base[0])
        real = jnp.concatenate([rows[2 * m : 2 * m + 1] for rows in collected], axis=0)
        imag = jnp.concatenate([rows[2 * m + 1 : 2 * m + 2] for rows in collected], axis=0)
        results.append((real * phase[0] + imag * phase[1], imag * phase[0] - real * phase[1]))
    for h in range(out_ref.shape[1]):
        for part in range(2):
            value = results[-1][part]
            for m in range(count - 1, 0, -1):
                value = jnp.where(harm_ref[h] == m, results[m - 1][part], value)
            out_ref[part, h] = value


def transform_table(instances, comps):
    orders = np.arange(1, 4)
    angles = 2.0 * np.pi * (orders[:, None] * np.arange(instances)[None, :] % instances) / instances
    real, imag = np.cos(angles) / instances, -np.sin(angles) / instances
    table = np.zeros((comps * 8, instances * comps), np.float64)
    for c in range(comps):
        for m in range(3):
            pair = (-imag[m], real[m]) if c == 0 else (real[m], imag[m])
            for part in range(2):
                table[c * 8 + 2 * m + part, c::comps] = pair[part]
    bf16 = jnp.bfloat16
    high = table.astype(bf16)
    middle = (table - high.astype(np.float64)).astype(bf16)
    low = (table - high.astype(np.float64) - middle.astype(np.float64)).astype(bf16)
    return np.stack([high, middle, low])


def per_device(
    sources, panel_positions, panel_copy, harmonic_numbers, blade_count, observer_ids, observer_radius, *, sizes,
):
    axes = ("inst", "panel", "obs")
    insts = sizes["inst"]
    devices = math.prod(sizes[axis] for axis in axes)
    per_inst, comps, own_panels = sources.shape
    rows = per_inst * comps + 8
    block_rows = observer_ids.shape[1] // (insts * sizes["panel"])
    observers = block_rows * LANES
    tiles = devices // insts * own_panels // TILE
    held = min(HELD_TILES, tiles)
    smem = pl.BlockSpec(memory_space=pltpu.SMEM)
    vmem = pl.BlockSpec(memory_space=pltpu.VMEM)

    block = pl.pallas_call(
        pack_kernel,
        out_shape=jax.ShapeDtypeStruct((devices, rows, own_panels), jnp.bfloat16),
        in_specs=[smem, vmem, vmem, vmem],
        out_specs=vmem,
        name="pack",
    )(blade_count, sources, panel_positions, panel_copy.reshape(1, own_panels))
    got = lax.all_to_all(block, axes, split_axis=0, concat_axis=0, tiled=True)
    table = jnp.asarray(transform_table(per_inst * insts, comps))
    kernel = functools.partial(main_kernel, insts=insts, per_inst=per_inst, comps=comps, orders=(1, 2, 3))
    harmonics = harmonic_numbers.shape[0]
    pressure = pl.pallas_call(
        kernel,
        out_shape=jax.ShapeDtypeStruct((2, harmonics, block_rows, LANES), jnp.float32),
        in_specs=[smem, smem, vmem, vmem, vmem, vmem],
        out_specs=vmem,
        scratch_shapes=[
            pltpu.VMEM((observers, DEPTH), jnp.bfloat16),
            pltpu.VMEM((observers, LANES), jnp.float32),
            pltpu.VMEM((13, held, DEPTH, TILE), jnp.bfloat16),
            pltpu.VMEM((6, observers, LANES), jnp.float32),
            pltpu.VMEM((TILE // LANES * FEATURES * 8, LANES), jnp.float32),
        ],
        name="panel_sum",
    )(harmonic_numbers, blade_count, table, got, observer_ids, observer_radius)
    return jnp.transpose(pressure, (2, 0, 1, 3))[None]


def solution(mesh):
    placed = (
        P("inst", None, ("panel", "obs")),
        P(None, ("panel", "obs")),
        P(("panel", "obs")),
        P(),
        P(),
        P("obs", None, None),
        P("obs", None, None),
    )
    return jax.shard_map(
        functools.partial(per_device, sizes=dict(mesh.shape)),
        mesh=mesh,
        in_specs=placed,
        out_specs=P("obs", ("inst", "panel"), None, None, None),
        check_vma=False,
    )
```

```python
import functools
import math

import jax
import jax.numpy as jnp
import numpy as np
from jax import lax
from jax.experimental import pallas as pl
from jax.experimental.pallas import tpu as pltpu
from jax.sharding import PartitionSpec as P

NTHETA = 256
NPHI = 512
WAVE_UNIT = 0.05
TWO_PI = 2.0 * 3.141592653589793
LANES = 128
TILE = 256
CHUNK = 512
HELD_TILES = 8
FEATURES = 8
PARTS = 6
DEPTH = FEATURES * PARTS

HALF_SINE = (6.28317247, -10.33464405, 5.08745911, -1.11966943)


def split_parts(value):
    high = value.astype(jnp.bfloat16).astype(jnp.float32)
    rest = value - high
    middle = rest.astype(jnp.bfloat16).astype(jnp.float32)
    return high, middle, rest - middle


def pack_kernel(blades_ref, src_ref, pos_ref, copy_ref, out_ref):
    inst_here = lax.axis_index("inst")
    angle = TWO_PI * copy_ref[...].astype(jnp.float32) / blades_ref[0].astype(jnp.float32)
    cosine, sine = jnp.cos(angle), jnp.sin(angle)
    x, y, z = pos_ref[0:1, :], pos_ref[1:2, :], pos_ref[2:3, :]
    values = (cosine * x - sine * y, sine * x + cosine * y, z, cosine, sine)
    parts = [split_parts(value) for value in values]
    rows = [parts[i][j] for j in range(3) for i in range(5)]
    rows.append(jnp.zeros_like(z))
    own = jnp.where(inst_here == 0, jnp.concatenate(rows[:8], axis=0), jnp.concatenate(rows[8:], axis=0))
    terms = [src_ref[n].astype(jnp.float32) for n in range(src_ref.shape[0])]
    block = jnp.concatenate(terms + [own], axis=0).astype(jnp.bfloat16)

    def put(d, carry):
        out_ref[d] = block
        return carry

    lax.fori_loop(0, out_ref.shape[0], put, 0)


def pair_factors(t2, t0, orders):
    w = lax.rsqrt(t2)
    w3 = w * (1.0 / t2)
    t = t2 * w
    f = t - t0
    z = f * f
    s = jnp.float32(HALF_SINE[-1])
    for c in HALF_SINE[-2::-1]:
        s = s * z + jnp.float32(c)
    s = s * f
    q = s * s
    twice = 2.0 - q
    d = 4.0 - q
    cosine = w3 * twice
    sine = w3 * (s * (1.0 / lax.rsqrt(d)))
    factors = {1: (cosine, sine)}
    if 2 in orders:
        factors[2] = (twice * cosine - (w3 + w3), twice * sine)
        if 3 in orders:
            factors[3] = (twice * factors[2][0] - cosine, twice * factors[2][1] - sine)
    elif 3 in orders:
        square = twice * twice
        factors[3] = (cosine * (square - 3.0), sine * (square - 1.0))
    return t, factors


def main_kernel(
    harm_ref, blades_ref, table_ref, got_ref, ids_ref, radius_ref, out_ref,
    feat_ref, hub_ref, coef_ref, acc_ref, rows_ref, *, insts, per_inst, comps, orders,
):
    block_rows = out_ref.shape[0]
    observers = block_rows * LANES
    groups = got_ref.shape[0] // insts
    tiles = groups * LANES // TILE
    held = min(HELD_TILES, tiles)
    per_tile = TILE // LANES
    src_rows = per_inst * comps
    count = len(orders)
    first = (lax.axis_index("inst") * lax.axis_size("panel") + lax.axis_index("panel")) * block_rows
    first = pl.multiple_of(first, 8)

    kappa = blades_ref[0].astype(jnp.float32) * WAVE_UNIT
    scale = kappa / TWO_PI

    ids = ids_ref[0, pl.ds(first, block_rows), :]
    radius = radius_ref[0, pl.ds(first, block_rows), :]
    theta = 3.141592653589793 * ((ids // NPHI).astype(jnp.float32) + 0.5) / NTHETA
    phi = TWO_PI * (ids % NPHI).astype(jnp.float32) / NPHI
    sine_theta = jnp.sin(theta)
    x1 = radius * sine_theta * jnp.cos(phi)
    x2 = radius * sine_theta * jnp.sin(phi)
    x3 = radius * jnp.cos(theta)
    hub = scale * radius
    features = (x1, x2, x3, jnp.ones_like(x1), radius * radius)
    for b in range(0, block_rows, 8):
        for i in range(FEATURES):
            value = features[i][b : b + 8] if i < len(features) else jnp.zeros((8, LANES), jnp.float32)
            rows_ref[i * 8 : (i + 1) * 8, :] = value
        for r in range(8):
            b1, b2, b3 = split_parts(rows_ref[pl.ds(r, FEATURES, stride=8), :])
            stack = [b1, b2, b3, b1, b2, b1, jnp.broadcast_to(hub[b + r : b + r + 1], (8, LANES))]
            stack.append(jnp.zeros((LANES - 8 * len(stack), LANES), jnp.float32))
            turned = jnp.concatenate(stack, axis=0).T
            at = slice((b + r) * LANES, (b + r + 1) * LANES)
            feat_ref[at, :] = turned[:, 0:DEPTH].astype(jnp.bfloat16)
            hub_ref[at, :] = jnp.broadcast_to(turned[:, DEPTH : DEPTH + 1], (LANES, LANES))

    row = lax.broadcasted_iota(jnp.int32, (8, TILE), 0)
    order_of_row = (row // 2 + 1).astype(jnp.float32)
    s2 = scale * scale
    s3 = s2 * scale
    far = s3 / (8.0 * 3.141592653589793)
    near = order_of_row * (s3 * 0.25)
    mono = order_of_row * (s2 * 0.25)

    def coefficients(first_tile):
        def one(j, carry):
            at = (first_tile + j) * per_tile
            src = [
                jnp.concatenate([got_ref[i * groups + at + p, 0:src_rows, :] for p in range(per_tile)], axis=1)
                for i in range(insts)
            ]
            src = jnp.concatenate(src, axis=0)
            spec = None
            for part in range(3):
                term = jnp.dot(table_ref[part], src, preferred_element_type=jnp.float32)
                spec = term if spec is None else spec + term
            turned_q, f1, f2, f3 = (spec[8 * c : 8 * c + 8] for c in range(4))
            geo = [
                jnp.concatenate(
                    [got_ref[i * groups + at + p, src_rows : src_rows + 8, :].astype(jnp.float32) for p in range(per_tile)],
                    axis=1,
                )
                for i in range(2)
            ]
            geo = [geo[i][r : r + 1] for i in range(2) for r in range(8)]
            y1, y2, y3, cosine, sine = (geo[i] + geo[5 + i] + geo[10 + i] for i in range(5))
            g1 = cosine * f1 - sine * f2
            g2 = sine * f1 + cosine * f2
            dipole = (g1, g2, f3, -(g1 * y1 + g2 * y2 + f3 * y3))
            square = y1 * y1 + y2 * y2 + y3 * y3
            distance = (-2.0 * s2 * y1, -2.0 * s2 * y2, -2.0 * s2 * y3, s2 * square, jnp.full_like(y1, s2))
            lifted = mono * turned_q
            zero = jnp.zeros((8, TILE), jnp.float32)

            def write(o, value):
                a1, a2, a3 = split_parts(value)
                coef_ref[o, j, 0:16, :] = jnp.concatenate([a1, a1], axis=0).astype(jnp.bfloat16)
                coef_ref[o, j, 16:32, :] = jnp.concatenate([a1, a2], axis=0).astype(jnp.bfloat16)
                coef_ref[o, j, 32:48, :] = jnp.concatenate([a2, a3], axis=0).astype(jnp.bfloat16)

            def keep(i, value):
                for p in range(per_tile):
                    rows_ref[(p * FEATURES + i) * 8 : (p * FEATURES + i + 1) * 8, :] = value[:, p * LANES : (p + 1) * LANES]

            def gathered(r):
                return jnp.concatenate(
                    [rows_ref[pl.ds(p * FEATURES * 8 + r, FEATURES, stride=8), :] for p in range(per_tile)], axis=1
                )

            write(0, jnp.concatenate(list(distance) + [zero[0:3]], axis=0))
            for i in range(FEATURES):
                value = zero
                if i < 4:
                    value = far * dipole[i] + lifted * distance[i]
                elif i == 4:
                    value = lifted * distance[i]
                keep(i, value)
            for m in range(3):
                for part in range(2):
                    write(1 + 4 * m + part, gathered(2 * m + part))
            for i in range(FEATURES):
                keep(i, near * dipole[i] if i < 4 else zero)
            for m in range(3):
                for part in range(2):
                    write(3 + 4 * m + part, gathered(2 * m + part))
            return carry

        lax.fori_loop(0, held, one, 0)

    def pair_sums(chosen):
        def step(it, carry):
            at = pl.multiple_of(it // held * CHUNK, CHUNK)
            j = it % held
            feat = feat_ref[pl.ds(at, CHUNK), :]

            def pair(o):
                return jnp.dot(feat, coef_ref[o, j], preferred_element_type=jnp.float32)

            squares = pair(0)
            pairs = {m: [pair(4 * m - 3 + i) for i in range(4)] for m in chosen}
            for v in range(CHUNK // 8):
                obs_rows = pl.ds(pl.multiple_of(at + v * 8, 8), 8)
                t0 = hub_ref[obs_rows, :]
                sums = {}
                for lane in range(TILE // LANES):
                    where = (slice(v * 8, v * 8 + 8), slice(lane * LANES, (lane + 1) * LANES))
                    t, factors = pair_factors(squares[where], t0, chosen)
                    for m in chosen:
                        cosine, sine = factors[m]
                        p_re, p_im, m_re, m_im = (matrix[where] for matrix in pairs[m])
                        real = p_re - t * m_im
                        imag = p_im + t * m_re
                        new = (cosine * real + sine * imag, cosine * imag - sine * real)
                        old = sums.get(m)
                        sums[m] = new if old is None else (old[0] + new[0], old[1] + new[1])
                for m in chosen:
                    for part in range(2):
                        o = 2 * (m - 1) + part
                        acc_ref[o, obs_rows, :] = acc_ref[o, obs_rows, :] + sums[m][part]
            return carry

        lax.fori_loop(0, observers // CHUNK * held, step, 0)

    acc_ref[...] = jnp.zeros_like(acc_ref)

    asked = [functools.reduce(jnp.logical_or, [harm_ref[h] == m for h in range(out_ref.shape[1])]) for m in orders]
    which = sum(jnp.where(present, 1 << i, 0) for i, present in enumerate(asked))

    def chunk(i, carry):
        coefficients(i * held)
        for bits in range(1, 1 << count):

            @pl.when(which == bits)
            def _():
                pair_sums(tuple(m for k, m in enumerate(orders) if bits >> k & 1))

        return carry

    lax.fori_loop(0, tiles // held, chunk, 0)

    turn = hub - jnp.round(hub)
    base = (jnp.cos(TWO_PI * turn), jnp.sin(TWO_PI * turn))
    lane_of = lax.broadcasted_iota(jnp.int32, (LANES, LANES), 1)
    collected = []
    for b in range(block_rows):
        matrix = jnp.zeros((LANES, LANES), jnp.float32)
        for o in range(2 * count):
            total = jnp.sum(acc_ref[o, b * LANES : (b + 1) * LANES, :], axis=1, keepdims=True)
            matrix = jnp.where(lane_of == o, total, matrix)
        collected.append(matrix.T[0:8])
    results = []
    phase = (jnp.ones_like(turn), jnp.zeros_like(turn))
    for m in range(count):
        phase = (phase[0] * base[0] - phase[1] * base[1], phase[0] * base[1] + phase[1] * base[0])
        real = jnp.concatenate([rows[2 * m : 2 * m + 1] for rows in collected], axis=0)
        imag = jnp.concatenate([rows[2 * m + 1 : 2 * m + 2] for rows in collected], axis=0)
        results.append((real * phase[0] + imag * phase[1], imag * phase[0] - real * phase[1]))
    for h in range(out_ref.shape[1]):
        for part in range(2):
            value = results[-1][part]
            for m in range(count - 1, 0, -1):
                value = jnp.where(harm_ref[h] == m, results[m - 1][part], value)
            out_ref[:, h, part, :] = value


def transform_table(instances, comps):
    orders = np.arange(1, 4)
    angles = 2.0 * np.pi * (orders[:, None] * np.arange(instances)[None, :] % instances) / instances
    real, imag = np.cos(angles) / instances, -np.sin(angles) / instances
    table = np.zeros((comps * 8, instances * comps), np.float64)
    for c in range(comps):
        for m in range(3):
            pair = (-imag[m], real[m]) if c == 0 else (real[m], imag[m])
            for part in range(2):
                table[c * 8 + 2 * m + part, c::comps] = pair[part]
    bf16 = jnp.bfloat16
    high = table.astype(bf16)
    middle = (table - high.astype(np.float64)).astype(bf16)
    low = (table - high.astype(np.float64) - middle.astype(np.float64)).astype(bf16)
    return np.stack([high, middle, low])


def per_device(
    sources, panel_positions, panel_copy, harmonic_numbers, blade_count, observer_ids, observer_radius, *, sizes,
):
    axes = ("inst", "panel", "obs")
    insts = sizes["inst"]
    devices = math.prod(sizes[axis] for axis in axes)
    per_inst, comps, own_panels = sources.shape
    rows = per_inst * comps + 8
    block_rows = observer_ids.shape[1] // (insts * sizes["panel"])
    observers = block_rows * LANES
    tiles = devices // insts * own_panels // TILE
    held = min(HELD_TILES, tiles)
    smem = pl.BlockSpec(memory_space=pltpu.SMEM)
    vmem = pl.BlockSpec(memory_space=pltpu.VMEM)

    block = pl.pallas_call(
        pack_kernel,
        out_shape=jax.ShapeDtypeStruct((devices, rows, own_panels), jnp.bfloat16),
        in_specs=[smem, vmem, vmem, vmem],
        out_specs=vmem,
        name="pack",
    )(blade_count, sources, panel_positions, panel_copy.reshape(1, own_panels))
    got = lax.all_to_all(block, axes, split_axis=0, concat_axis=0, tiled=True)
    table = jnp.asarray(transform_table(per_inst * insts, comps))
    kernel = functools.partial(main_kernel, insts=insts, per_inst=per_inst, comps=comps, orders=(1, 2, 3))
    harmonics = harmonic_numbers.shape[0]
    pressure = pl.pallas_call(
        kernel,
        out_shape=jax.ShapeDtypeStruct((block_rows, harmonics, 2, LANES), jnp.float32),
        in_specs=[smem, smem, vmem, vmem, vmem, vmem],
        out_specs=vmem,
        scratch_shapes=[
            pltpu.VMEM((observers, DEPTH), jnp.bfloat16),
            pltpu.VMEM((observers, LANES), jnp.float32),
            pltpu.VMEM((13, held, DEPTH, TILE), jnp.bfloat16),
            pltpu.VMEM((6, observers, LANES), jnp.float32),
            pltpu.VMEM((TILE // LANES * FEATURES * 8, LANES), jnp.float32),
        ],
        name="panel_sum",
    )(harmonic_numbers, blade_count, table, got, observer_ids, observer_radius)
    return jnp.transpose(pressure, (0, 2, 1, 3))[None]


def solution(mesh):
    placed = (
        P("inst", None, ("panel", "obs")),
        P(None, ("panel", "obs")),
        P(("panel", "obs")),
        P(),
        P(),
        P("obs", None, None),
        P("obs", None, None),
    )
    return jax.shard_map(
        functools.partial(per_device, sizes=dict(mesh.shape)),
        mesh=mesh,
        in_specs=placed,
        out_specs=P("obs", ("inst", "panel"), None, None, None),
        check_vma=False,
    )
```

```python
import functools
import math

import jax
import jax.numpy as jnp
import numpy as np
from jax import lax
from jax.experimental import pallas as pl
from jax.experimental.pallas import tpu as pltpu
from jax.sharding import PartitionSpec as P

NTHETA = 256
NPHI = 512
WAVE_UNIT = 0.05
TWO_PI = 2.0 * 3.141592653589793
LANES = 128
TILE = 256
CHUNK = 512
HELD_TILES = 8
FEATURES = 8
PARTS = 6
DEPTH = FEATURES * PARTS

UNIT = 1.0162787191656768
HALF_SINE = (6.182528619811836, -9.84593645135278, 4.692851090969603)


def split_parts(value):
    high = value.astype(jnp.bfloat16).astype(jnp.float32)
    rest = value - high
    middle = rest.astype(jnp.bfloat16).astype(jnp.float32)
    return high, middle, rest - middle


def pack_kernel(blades_ref, src_ref, pos_ref, copy_ref, out_ref, scale_ref):
    inst_here = lax.axis_index("inst")
    scale_ref[...] = jnp.full(scale_ref.shape, blades_ref[0].astype(jnp.float32) * WAVE_UNIT / TWO_PI)
    angle = TWO_PI * copy_ref[...].astype(jnp.float32) / blades_ref[0].astype(jnp.float32)
    cosine, sine = jnp.cos(angle), jnp.sin(angle)
    x, y, z = pos_ref[0:1, :], pos_ref[1:2, :], pos_ref[2:3, :]
    values = (cosine * x - sine * y, sine * x + cosine * y, z, cosine, sine)
    parts = [split_parts(value) for value in values]
    rows = [parts[i][j] for j in range(3) for i in range(5)]
    rows.append(jnp.zeros_like(z))
    own = jnp.where(inst_here == 0, jnp.concatenate(rows[:8], axis=0), jnp.concatenate(rows[8:], axis=0))
    terms = [src_ref[n].astype(jnp.float32) for n in range(src_ref.shape[0])]
    block = jnp.concatenate(terms + [own], axis=0).astype(jnp.bfloat16)

    def put(d, carry):
        out_ref[d] = block
        return carry

    lax.fori_loop(0, out_ref.shape[0], put, 0)


def pair_factors(t2, t0, orders):
    w = lax.rsqrt(t2)
    w3 = w * (1.0 / t2)
    t = t2 * w
    f = t - t0
    z = f * f
    s = jnp.float32(HALF_SINE[2]) - z
    for c in HALF_SINE[1::-1]:
        s = s * z + jnp.float32(c)
    s = s * f
    q = s * s
    twice = 2.0 - q
    d = 4.0 - q
    cosine = w3 * twice
    sine = w3 * (s * (1.0 / lax.rsqrt(d)))
    factors = {1: (cosine, sine)}
    if 2 in orders:
        factors[2] = (twice * cosine - (w3 + w3), twice * sine)
        if 3 in orders:
            factors[3] = (twice * factors[2][0] - cosine, twice * factors[2][1] - sine)
    elif 3 in orders:
        square = twice * twice
        factors[3] = (cosine * (square - 3.0), sine * (square - 1.0))
    return t, factors


def observer_kernel(harm_ref, scale_ref, ids_ref, radius_ref, feat_ref, hub_ref, dense_ref, harm_rows_ref, rows_ref):
    block_rows = dense_ref.shape[0]
    first = (lax.axis_index("inst") * lax.axis_size("panel") + lax.axis_index("panel")) * block_rows
    first = pl.multiple_of(first, 8)

    ids = ids_ref[0, pl.ds(first, block_rows), :]
    radius = radius_ref[0, pl.ds(first, block_rows), :]
    theta = 3.141592653589793 * ((ids // NPHI).astype(jnp.float32) + 0.5) / NTHETA
    phi = TWO_PI * (ids % NPHI).astype(jnp.float32) / NPHI
    sine_theta = jnp.sin(theta)
    x1 = radius * sine_theta * jnp.cos(phi)
    x2 = radius * sine_theta * jnp.sin(phi)
    x3 = radius * jnp.cos(theta)
    hub = UNIT * scale_ref[0:1, :] * radius
    dense_ref[...] = hub
    for h in range(harm_rows_ref.shape[0]):
        harm_rows_ref[h] = jnp.full((8, LANES), harm_ref[h].astype(jnp.float32))
    features = (x1, x2, x3, jnp.ones_like(x1), radius * radius)
    for b in range(0, block_rows, 8):
        for i in range(FEATURES):
            value = features[i][b : b + 8] if i < len(features) else jnp.zeros((8, LANES), jnp.float32)
            rows_ref[i * 8 : (i + 1) * 8, :] = value
        for r in range(8):
            b1, b2, b3 = split_parts(rows_ref[pl.ds(r, FEATURES, stride=8), :])
            stack = [b1, b2, b3, b1, b2, b1, jnp.broadcast_to(hub[b + r : b + r + 1], (8, LANES))]
            stack.append(jnp.zeros((LANES - 8 * len(stack), LANES), jnp.float32))
            turned = jnp.concatenate(stack, axis=0).T
            at = slice((b + r) * LANES, (b + r + 1) * LANES)
            feat_ref[at, :] = turned[:, 0:DEPTH].astype(jnp.bfloat16)
            hub_ref[at, :] = jnp.broadcast_to(turned[:, DEPTH : DEPTH + 1], (LANES, LANES))


def main_kernel(
    table_ref, got_ref, scale_ref, harm_rows_ref, feat_ref, hub_ref, dense_ref, out_ref,
    coef_ref, acc_ref, rows_ref, *, insts, per_inst, comps, orders,
):
    block_rows = out_ref.shape[0]
    observers = block_rows * LANES
    groups = got_ref.shape[0] // insts
    tiles = groups * LANES // TILE
    held = min(HELD_TILES, tiles)
    per_tile = TILE // LANES
    src_rows = per_inst * comps
    count = len(orders)
    scale = jnp.concatenate([scale_ref[...]] * (TILE // LANES), axis=1)
    unit = UNIT * scale
    row = lax.broadcasted_iota(jnp.int32, (8, TILE), 0)
    order_of_row = (row // 2 + 1).astype(jnp.float32)
    s2 = unit * unit
    far = s2 * unit / (8.0 * 3.141592653589793)
    near = order_of_row * (s2 * scale * 0.25)
    mono = order_of_row * (unit * scale * 0.25)

    def coefficients(first_tile):
        def one(j, carry):
            at = (first_tile + j) * per_tile
            src = [
                jnp.concatenate([got_ref[i * groups + at + p, 0:src_rows, :] for p in range(per_tile)], axis=1)
                for i in range(insts)
            ]
            src = jnp.concatenate(src, axis=0)
            spec = None
            for part in range(3):
                term = jnp.dot(table_ref[part], src, preferred_element_type=jnp.float32)
                spec = term if spec is None else spec + term
            turned_q, f1, f2, f3 = (spec[8 * c : 8 * c + 8] for c in range(4))
            geo = [
                jnp.concatenate(
                    [got_ref[i * groups + at + p, src_rows : src_rows + 8, :].astype(jnp.float32) for p in range(per_tile)],
                    axis=1,
                )
                for i in range(2)
            ]
            geo = [geo[i][r : r + 1] for i in range(2) for r in range(8)]
            y1, y2, y3, cosine, sine = (geo[i] + geo[5 + i] + geo[10 + i] for i in range(5))
            g1 = cosine * f1 - sine * f2
            g2 = sine * f1 + cosine * f2
            dipole = (g1, g2, f3, -(g1 * y1 + g2 * y2 + f3 * y3))
            square = y1 * y1 + y2 * y2 + y3 * y3
            row2 = s2[0:1, :]
            distance = (-2.0 * row2 * y1, -2.0 * row2 * y2, -2.0 * row2 * y3, row2 * square, row2)
            lifted = mono * turned_q
            zero = jnp.zeros((8, TILE), jnp.float32)

            def write(o, value):
                a1, a2, a3 = split_parts(value)
                coef_ref[o, j, 0:16, :] = jnp.concatenate([a1, a1], axis=0).astype(jnp.bfloat16)
                coef_ref[o, j, 16:32, :] = jnp.concatenate([a1, a2], axis=0).astype(jnp.bfloat16)
                coef_ref[o, j, 32:48, :] = jnp.concatenate([a2, a3], axis=0).astype(jnp.bfloat16)

            def keep(i, value):
                for p in range(per_tile):
                    rows_ref[(p * FEATURES + i) * 8 : (p * FEATURES + i + 1) * 8, :] = value[:, p * LANES : (p + 1) * LANES]

            def gathered(r):
                return jnp.concatenate(
                    [rows_ref[pl.ds(p * FEATURES * 8 + r, FEATURES, stride=8), :] for p in range(per_tile)], axis=1
                )

            write(0, jnp.concatenate(list(distance) + [zero[0:3]], axis=0))
            for i in range(FEATURES):
                value = zero
                if i < 4:
                    value = far * dipole[i] + lifted * distance[i]
                elif i == 4:
                    value = lifted * distance[i]
                keep(i, value)
            for m in range(3):
                for part in range(2):
                    write(1 + 4 * m + part, gathered(2 * m + part))
            for i in range(FEATURES):
                keep(i, near * dipole[i] if i < 4 else zero)
            for m in range(3):
                for part in range(2):
                    write(3 + 4 * m + part, gathered(2 * m + part))
            return carry

        lax.fori_loop(0, held, one, 0)

    def pair_sums(chosen):
        def step(it, carry):
            at = pl.multiple_of(it // held * CHUNK, CHUNK)
            j = it % held
            feat = feat_ref[pl.ds(at, CHUNK), :]

            def pair(o):
                return jnp.dot(feat, coef_ref[o, j], preferred_element_type=jnp.float32)

            squares = pair(0)
            pairs = {m: [pair(4 * m - 3 + i) for i in range(4)] for m in chosen}
            for v in range(CHUNK // 8):
                obs_rows = pl.ds(pl.multiple_of(at + v * 8, 8), 8)
                t0 = hub_ref[obs_rows, :]
                sums = {}
                for lane in range(TILE // LANES):
                    where = (slice(v * 8, v * 8 + 8), slice(lane * LANES, (lane + 1) * LANES))
                    t, factors = pair_factors(squares[where], t0, chosen)
                    for m in chosen:
                        cosine, sine = factors[m]
                        p_re, p_im, m_re, m_im = (matrix[where] for matrix in pairs[m])
                        real = p_re - t * m_im
                        imag = p_im + t * m_re
                        new = (cosine * real + sine * imag, cosine * imag - sine * real)
                        old = sums.get(m)
                        sums[m] = new if old is None else (old[0] + new[0], old[1] + new[1])
                for m in chosen:
                    for part in range(2):
                        o = 2 * (m - 1) + part
                        acc_ref[o, obs_rows, :] = acc_ref[o, obs_rows, :] + sums[m][part]
            return carry

        lax.fori_loop(0, observers // CHUNK * held, step, 0)

    acc_ref[...] = jnp.zeros_like(acc_ref)

    harm = [harm_rows_ref[h] for h in range(out_ref.shape[1])]
    asked = [functools.reduce(jnp.logical_or, [rows == m for rows in harm]) for m in orders]
    bits_of = sum(jnp.where(present, float(1 << i), 0.0) for i, present in enumerate(asked))
    which = jnp.max(bits_of).astype(jnp.int32)

    def chunk(i, carry):
        coefficients(i * held)
        for bits in range(1, 1 << count):

            @pl.when(which == bits)
            def _():
                pair_sums(tuple(m for k, m in enumerate(orders) if bits >> k & 1))

        return carry

    lax.fori_loop(0, tiles // held, chunk, 0)

    turn = dense_ref[...] * (1.0 / UNIT)
    turn = turn - jnp.round(turn)
    base = (jnp.cos(TWO_PI * turn), jnp.sin(TWO_PI * turn))
    lane_of = lax.broadcasted_iota(jnp.int32, (LANES, LANES), 1)
    collected = []
    for b in range(block_rows):
        matrix = jnp.zeros((LANES, LANES), jnp.float32)
        for o in range(2 * count):
            total = jnp.sum(acc_ref[o, b * LANES : (b + 1) * LANES, :], axis=1, keepdims=True)
            matrix = jnp.where(lane_of == o, total, matrix)
        collected.append(matrix.T[0:8])
    results = []
    phase = (jnp.ones_like(turn), jnp.zeros_like(turn))
    for m in range(count):
        phase = (phase[0] * base[0] - phase[1] * base[1], phase[0] * base[1] + phase[1] * base[0])
        real = jnp.concatenate([rows[2 * m : 2 * m + 1] for rows in collected], axis=0)
        imag = jnp.concatenate([rows[2 * m + 1 : 2 * m + 2] for rows in collected], axis=0)
        results.append((real * phase[0] + imag * phase[1], imag * phase[0] - real * phase[1]))
    def harm_of(h):
        return harm_rows_ref[h, 0:1, :]

    for h in range(out_ref.shape[1]):
        for part in range(2):
            value = results[-1][part]
            for m in range(count - 1, 0, -1):
                value = jnp.where(harm_of(h) == m, results[m - 1][part], value)
            out_ref[:, h, part, :] = value


def transform_table(instances, comps):
    orders = np.arange(1, 4)
    angles = 2.0 * np.pi * (orders[:, None] * np.arange(instances)[None, :] % instances) / instances
    real, imag = np.cos(angles) / instances, -np.sin(angles) / instances
    table = np.zeros((comps * 8, instances * comps), np.float64)
    for c in range(comps):
        for m in range(3):
            pair = (-imag[m], real[m]) if c == 0 else (real[m], imag[m])
            for part in range(2):
                table[c * 8 + 2 * m + part, c::comps] = pair[part]
    bf16 = jnp.bfloat16
    high = table.astype(bf16)
    middle = (table - high.astype(np.float64)).astype(bf16)
    low = (table - high.astype(np.float64) - middle.astype(np.float64)).astype(bf16)
    return np.stack([high, middle, low])


def per_device(
    sources, panel_positions, panel_copy, harmonic_numbers, blade_count, observer_ids, observer_radius, *, sizes,
):
    axes = ("inst", "panel", "obs")
    insts = sizes["inst"]
    devices = math.prod(sizes[axis] for axis in axes)
    per_inst, comps, own_panels = sources.shape
    rows = per_inst * comps + 8
    block_rows = observer_ids.shape[1] // (insts * sizes["panel"])
    observers = block_rows * LANES
    tiles = devices // insts * own_panels // TILE
    held = min(HELD_TILES, tiles)
    smem = pl.BlockSpec(memory_space=pltpu.SMEM)
    vmem = pl.BlockSpec(memory_space=pltpu.VMEM)

    block, scale = pl.pallas_call(
        pack_kernel,
        out_shape=[
            jax.ShapeDtypeStruct((devices, rows, own_panels), jnp.bfloat16),
            jax.ShapeDtypeStruct((8, LANES), jnp.float32),
        ],
        in_specs=[smem, vmem, vmem, vmem],
        out_specs=[vmem, vmem],
        name="pack",
    )(blade_count, sources, panel_positions, panel_copy.reshape(1, own_panels))
    got = lax.all_to_all(block, axes, split_axis=0, concat_axis=0, tiled=True)
    table = jnp.asarray(transform_table(per_inst * insts, comps))
    kernel = functools.partial(main_kernel, insts=insts, per_inst=per_inst, comps=comps, orders=(1, 2, 3))
    harmonics = harmonic_numbers.shape[0]
    feat, hub, dense, harm_rows = pl.pallas_call(
        observer_kernel,
        out_shape=[
            jax.ShapeDtypeStruct((observers, DEPTH), jnp.bfloat16),
            jax.ShapeDtypeStruct((observers, LANES), jnp.float32),
            jax.ShapeDtypeStruct((block_rows, LANES), jnp.float32),
            jax.ShapeDtypeStruct((harmonics, 8, LANES), jnp.float32),
        ],
        in_specs=[smem, vmem, vmem, vmem],
        out_specs=[vmem] * 4,
        scratch_shapes=[pltpu.VMEM((8 * FEATURES, LANES), jnp.float32)],
        cost_estimate=pl.CostEstimate(flops=10_000_000, bytes_accessed=1_000_000, transcendentals=0),
        compiler_params=pltpu.CompilerParams(vmem_limit_bytes=8 << 20),
        name="observers",
    )(harmonic_numbers, scale, observer_ids, observer_radius)
    pressure = pl.pallas_call(
        kernel,
        out_shape=jax.ShapeDtypeStruct((block_rows, harmonics, 2, LANES), jnp.float32),
        in_specs=[vmem] * 7,
        out_specs=vmem,
        scratch_shapes=[
            pltpu.VMEM((13, held, DEPTH, TILE), jnp.bfloat16),
            pltpu.VMEM((6, observers, LANES), jnp.float32),
            pltpu.VMEM((TILE // LANES * FEATURES * 8, LANES), jnp.float32),
        ],
        compiler_params=pltpu.CompilerParams(vmem_limit_bytes=32 << 20),
        name="panel_sum",
    )(table, got, scale, harm_rows, feat, hub, dense)
    return jnp.transpose(pressure, (0, 2, 1, 3))[None]


def solution(mesh):
    placed = (
        P("inst", None, ("panel", "obs")),
        P(None, ("panel", "obs")),
        P(("panel", "obs")),
        P(),
        P(),
        P("obs", None, None),
        P("obs", None, None),
    )
    return jax.shard_map(
        functools.partial(per_device, sizes=dict(mesh.shape)),
        mesh=mesh,
        in_specs=placed,
        out_specs=P("obs", ("inst", "panel"), None, None, None),
        check_vma=False,
    )
```

```python
import functools
import math

import jax
import jax.numpy as jnp
import numpy as np
from jax import lax
from jax.experimental import pallas as pl
from jax.experimental.pallas import tpu as pltpu
from jax.sharding import PartitionSpec as P

NTHETA = 256
NPHI = 512
WAVE_UNIT = 0.05
TWO_PI = 2.0 * 3.141592653589793
LANES = 128
TILE = 256
CHUNK = 512
HELD_TILES = 8
FEATURES = 8
PARTS = 6
DEPTH = FEATURES * PARTS

UNIT = 1.0162787191656768
HALF_SINE = (6.182528619811836, -9.84593645135278, 4.692851090969603)


def split_parts(value):
    high = value.astype(jnp.bfloat16).astype(jnp.float32)
    rest = value - high
    middle = rest.astype(jnp.bfloat16).astype(jnp.float32)
    return high, middle, rest - middle


def pack_kernel(blades_ref, src_ref, pos_ref, copy_ref, out_ref, scale_ref):
    inst_here = lax.axis_index("inst")
    blades = jnp.broadcast_to(blades_ref[...].astype(jnp.float32), (1, LANES))
    scale_ref[...] = jnp.broadcast_to(blades * WAVE_UNIT / TWO_PI, scale_ref.shape)
    angle = TWO_PI * copy_ref[...].astype(jnp.float32) / blades
    cosine, sine = jnp.cos(angle), jnp.sin(angle)
    x, y, z = pos_ref[0:1, :], pos_ref[1:2, :], pos_ref[2:3, :]
    values = (cosine * x - sine * y, sine * x + cosine * y, z, cosine, sine)
    parts = [split_parts(value) for value in values]
    rows = [parts[i][j] for j in range(3) for i in range(5)]
    rows.append(jnp.zeros_like(z))
    own = jnp.where(inst_here == 0, jnp.concatenate(rows[:8], axis=0), jnp.concatenate(rows[8:], axis=0))
    terms = [src_ref[n].astype(jnp.float32) for n in range(src_ref.shape[0])]
    block = jnp.concatenate(terms + [own], axis=0).astype(jnp.bfloat16)

    def put(d, carry):
        out_ref[d] = block
        return carry

    lax.fori_loop(0, out_ref.shape[0], put, 0)


def pair_factors(t2, t0, orders):
    w = lax.rsqrt(t2)
    w3 = w * (1.0 / t2)
    t = t2 * w
    f = t - t0
    z = f * f
    s = jnp.float32(HALF_SINE[2]) - z
    for c in HALF_SINE[1::-1]:
        s = s * z + jnp.float32(c)
    s = s * f
    q = s * s
    twice = 2.0 - q
    d = 4.0 - q
    cosine = w3 * twice
    sine = w3 * (s * (1.0 / lax.rsqrt(d)))
    factors = {1: (cosine, sine)}
    if 2 in orders:
        factors[2] = (twice * cosine - (w3 + w3), twice * sine)
        if 3 in orders:
            factors[3] = (twice * factors[2][0] - cosine, twice * factors[2][1] - sine)
    elif 3 in orders:
        square = twice * twice
        factors[3] = (cosine * (square - 3.0), sine * (square - 1.0))
    return t, factors


def observer_kernel(harm_ref, scale_ref, ids_ref, radius_ref, feat_ref, hub_ref, dense_ref, harm_rows_ref, rows_ref):
    block_rows = dense_ref.shape[0]
    first = (lax.axis_index("inst") * lax.axis_size("panel") + lax.axis_index("panel")) * block_rows
    first = pl.multiple_of(first, 8)

    ids = ids_ref[0, pl.ds(first, block_rows), :]
    radius = radius_ref[0, pl.ds(first, block_rows), :]
    theta = 3.141592653589793 * ((ids // NPHI).astype(jnp.float32) + 0.5) / NTHETA
    phi = TWO_PI * (ids % NPHI).astype(jnp.float32) / NPHI
    sine_theta = jnp.sin(theta)
    x1 = radius * sine_theta * jnp.cos(phi)
    x2 = radius * sine_theta * jnp.sin(phi)
    x3 = radius * jnp.cos(theta)
    hub = UNIT * scale_ref[0:1, :] * radius
    dense_ref[...] = hub
    for h in range(harm_rows_ref.shape[0]):
        harm_rows_ref[h] = jnp.full((8, LANES), harm_ref[h].astype(jnp.float32))
    features = (x1, x2, x3, jnp.ones_like(x1), radius * radius)
    for b in range(0, block_rows, 8):
        for i in range(FEATURES):
            value = features[i][b : b + 8] if i < len(features) else jnp.zeros((8, LANES), jnp.float32)
            rows_ref[i * 8 : (i + 1) * 8, :] = value
        for r in range(8):
            b1, b2, b3 = split_parts(rows_ref[pl.ds(r, FEATURES, stride=8), :])
            stack = [b1, b2, b3, b1, b2, b1, jnp.broadcast_to(hub[b + r : b + r + 1], (8, LANES))]
            stack.append(jnp.zeros((LANES - 8 * len(stack), LANES), jnp.float32))
            turned = jnp.concatenate(stack, axis=0).T
            at = slice((b + r) * LANES, (b + r + 1) * LANES)
            feat_ref[at, :] = turned[:, 0:DEPTH].astype(jnp.bfloat16)
            hub_ref[at, :] = jnp.broadcast_to(turned[:, DEPTH : DEPTH + 1], (LANES, LANES))


def main_kernel(
    table_ref, got_ref, scale_ref, harm_rows_ref, feat_ref, hub_ref, dense_ref, out_ref,
    coef_ref, acc_ref, rows_ref, total_ref, *, insts, per_inst, comps, orders,
):
    block_rows = out_ref.shape[0]
    observers = block_rows * LANES
    groups = got_ref.shape[0] // insts
    tiles = groups * LANES // TILE
    held = min(HELD_TILES, tiles)
    per_tile = TILE // LANES
    src_rows = per_inst * comps
    count = len(orders)
    scale = jnp.concatenate([scale_ref[...]] * (TILE // LANES), axis=1)
    unit = UNIT * scale
    row = lax.broadcasted_iota(jnp.int32, (8, TILE), 0)
    order_of_row = (row // 2 + 1).astype(jnp.float32)
    s2 = unit * unit
    far = s2 * unit / (8.0 * 3.141592653589793)
    near = order_of_row * (s2 * scale * 0.25)
    mono = order_of_row * (unit * scale * 0.25)

    def coefficients(first_tile):
        def one(j, carry):
            at = (first_tile + j) * per_tile
            src = [
                jnp.concatenate([got_ref[i * groups + at + p, 0:src_rows, :] for p in range(per_tile)], axis=1)
                for i in range(insts)
            ]
            src = jnp.concatenate(src, axis=0)
            spec = None
            for part in range(3):
                term = jnp.dot(table_ref[part], src, preferred_element_type=jnp.float32)
                spec = term if spec is None else spec + term
            turned_q, f1, f2, f3 = (spec[8 * c : 8 * c + 8] for c in range(4))
            geo = [
                jnp.concatenate(
                    [got_ref[i * groups + at + p, src_rows : src_rows + 8, :].astype(jnp.float32) for p in range(per_tile)],
                    axis=1,
                )
                for i in range(2)
            ]
            geo = [geo[i][r : r + 1] for i in range(2) for r in range(8)]
            y1, y2, y3, cosine, sine = (geo[i] + geo[5 + i] + geo[10 + i] for i in range(5))
            g1 = cosine * f1 - sine * f2
            g2 = sine * f1 + cosine * f2
            dipole = (g1, g2, f3, -(g1 * y1 + g2 * y2 + f3 * y3))
            square = y1 * y1 + y2 * y2 + y3 * y3
            row2 = s2[0:1, :]
            distance = (-2.0 * row2 * y1, -2.0 * row2 * y2, -2.0 * row2 * y3, row2 * square, row2)
            lifted = mono * turned_q
            zero = jnp.zeros((8, TILE), jnp.float32)

            def write(o, value):
                a1, a2, a3 = split_parts(value)
                coef_ref[o, j, 0:16, :] = jnp.concatenate([a1, a1], axis=0).astype(jnp.bfloat16)
                coef_ref[o, j, 16:32, :] = jnp.concatenate([a1, a2], axis=0).astype(jnp.bfloat16)
                coef_ref[o, j, 32:48, :] = jnp.concatenate([a2, a3], axis=0).astype(jnp.bfloat16)

            def keep(i, value):
                for p in range(per_tile):
                    rows_ref[(p * FEATURES + i) * 8 : (p * FEATURES + i + 1) * 8, :] = value[:, p * LANES : (p + 1) * LANES]

            def gathered(r):
                return jnp.concatenate(
                    [rows_ref[pl.ds(p * FEATURES * 8 + r, FEATURES, stride=8), :] for p in range(per_tile)], axis=1
                )

            write(0, jnp.concatenate(list(distance) + [zero[0:3]], axis=0))
            for i in range(FEATURES):
                value = zero
                if i < 4:
                    value = far * dipole[i] + lifted * distance[i]
                elif i == 4:
                    value = lifted * distance[i]
                keep(i, value)
            for m in range(3):
                for part in range(2):
                    write(1 + 4 * m + part, gathered(2 * m + part))
            for i in range(FEATURES):
                keep(i, near * dipole[i] if i < 4 else zero)
            for m in range(3):
                for part in range(2):
                    write(3 + 4 * m + part, gathered(2 * m + part))
            return carry

        lax.fori_loop(0, held, one, 0)

    def pair_sums(chosen):
        def step(it, carry):
            at = pl.multiple_of(it // held * CHUNK, CHUNK)
            j = it % held
            feat = feat_ref[pl.ds(at, CHUNK), :]

            def pair(o):
                return jnp.dot(feat, coef_ref[o, j], preferred_element_type=jnp.float32)

            squares = pair(0)
            pairs = {m: [pair(4 * m - 3 + i) for i in range(4)] for m in chosen}
            for v in range(CHUNK // 8):
                obs_rows = pl.ds(pl.multiple_of(at + v * 8, 8), 8)
                t0 = hub_ref[obs_rows, :]
                sums = {}
                for lane in range(TILE // LANES):
                    where = (slice(v * 8, v * 8 + 8), slice(lane * LANES, (lane + 1) * LANES))
                    t, factors = pair_factors(squares[where], t0, chosen)
                    for m in chosen:
                        cosine, sine = factors[m]
                        p_re, p_im, m_re, m_im = (matrix[where] for matrix in pairs[m])
                        real = p_re - t * m_im
                        imag = p_im + t * m_re
                        new = (cosine * real + sine * imag, cosine * imag - sine * real)
                        old = sums.get(m)
                        sums[m] = new if old is None else (old[0] + new[0], old[1] + new[1])
                for m in chosen:
                    for part in range(2):
                        o = 2 * (m - 1) + part
                        acc_ref[o, obs_rows, :] = acc_ref[o, obs_rows, :] + sums[m][part]
            return carry

        lax.fori_loop(0, observers // CHUNK * held, step, 0)

    harm = [harm_rows_ref[h] for h in range(out_ref.shape[1])]
    asked = [functools.reduce(jnp.logical_or, [rows == m for rows in harm]) for m in orders]
    bits_of = sum(jnp.where(present, float(1 << i), 0.0) for i, present in enumerate(asked))
    which = jnp.max(bits_of).astype(jnp.int32)
    for i in range(count):

        @pl.when((which >> i) & 1 == 1)
        def _():
            acc_ref[2 * i : 2 * i + 2] = jnp.zeros((2,) + acc_ref.shape[1:], jnp.float32)


    def chunk(i, carry):
        coefficients(i * held)
        for bits in range(1, 1 << count):

            @pl.when(which == bits)
            def _():
                pair_sums(tuple(m for k, m in enumerate(orders) if bits >> k & 1))

        return carry

    lax.fori_loop(0, tiles // held, chunk, 0)

    turn = dense_ref[...] * (1.0 / UNIT)
    turn = turn - jnp.round(turn)
    base = (jnp.cos(TWO_PI * turn), jnp.sin(TWO_PI * turn))

    def collected(o):
        parts = [acc_ref[o, b * LANES : (b + 1) * LANES, :].T for b in range(block_rows)]
        return jnp.concatenate([jnp.sum(part, axis=0, keepdims=True) for part in parts], axis=0)

    for i in range(count):

        @pl.when((which >> i) & 1 == 1)
        def _():
            for o in (2 * i, 2 * i + 1):
                total_ref[o] = collected(o)

    results = []
    phase = (jnp.ones_like(turn), jnp.zeros_like(turn))
    for m in range(count):
        phase = (phase[0] * base[0] - phase[1] * base[1], phase[0] * base[1] + phase[1] * base[0])
        real, imag = total_ref[2 * m], total_ref[2 * m + 1]
        results.append((real * phase[0] + imag * phase[1], imag * phase[0] - real * phase[1]))

    def harm_of(h):
        return harm_rows_ref[h, 0:1, :]

    for h in range(out_ref.shape[1]):
        for part in range(2):
            value = results[-1][part]
            for m in range(count - 1, 0, -1):
                value = jnp.where(harm_of(h) == m, results[m - 1][part], value)
            out_ref[:, h, part, :] = value


def transform_table(instances, comps):
    orders = np.arange(1, 4)
    angles = 2.0 * np.pi * (orders[:, None] * np.arange(instances)[None, :] % instances) / instances
    real, imag = np.cos(angles) / instances, -np.sin(angles) / instances
    table = np.zeros((comps * 8, instances * comps), np.float64)
    for c in range(comps):
        for m in range(3):
            pair = (-imag[m], real[m]) if c == 0 else (real[m], imag[m])
            for part in range(2):
                table[c * 8 + 2 * m + part, c::comps] = pair[part]
    bf16 = jnp.bfloat16
    high = table.astype(bf16)
    middle = (table - high.astype(np.float64)).astype(bf16)
    low = (table - high.astype(np.float64) - middle.astype(np.float64)).astype(bf16)
    return np.stack([high, middle, low])


def per_device(
    sources, panel_positions, panel_copy, harmonic_numbers, blade_count, observer_ids, observer_radius, *, sizes,
):
    axes = ("inst", "panel", "obs")
    insts = sizes["inst"]
    devices = math.prod(sizes[axis] for axis in axes)
    per_inst, comps, own_panels = sources.shape
    rows = per_inst * comps + 8
    block_rows = observer_ids.shape[1] // (insts * sizes["panel"])
    observers = block_rows * LANES
    tiles = devices // insts * own_panels // TILE
    held = min(HELD_TILES, tiles)
    smem = pl.BlockSpec(memory_space=pltpu.SMEM)
    vmem = pl.BlockSpec(memory_space=pltpu.VMEM)

    block, scale = pl.pallas_call(
        pack_kernel,
        out_shape=[
            jax.ShapeDtypeStruct((devices, rows, own_panels), jnp.bfloat16),
            jax.ShapeDtypeStruct((8, LANES), jnp.float32),
        ],
        in_specs=[vmem] * 4,
        out_specs=[vmem, vmem],
        name="pack",
    )(blade_count.reshape(1, 1), sources, panel_positions, panel_copy.reshape(1, own_panels))
    got = lax.all_to_all(block, axes, split_axis=0, concat_axis=0, tiled=True)
    table = jnp.asarray(transform_table(per_inst * insts, comps))
    kernel = functools.partial(main_kernel, insts=insts, per_inst=per_inst, comps=comps, orders=(1, 2, 3))
    harmonics = harmonic_numbers.shape[0]
    feat, hub, dense, harm_rows = pl.pallas_call(
        observer_kernel,
        out_shape=[
            jax.ShapeDtypeStruct((observers, DEPTH), jnp.bfloat16),
            jax.ShapeDtypeStruct((observers, LANES), jnp.float32),
            jax.ShapeDtypeStruct((block_rows, LANES), jnp.float32),
            jax.ShapeDtypeStruct((harmonics, 8, LANES), jnp.float32),
        ],
        in_specs=[smem, vmem, vmem, vmem],
        out_specs=[vmem] * 4,
        scratch_shapes=[pltpu.VMEM((8 * FEATURES, LANES), jnp.float32)],
        cost_estimate=pl.CostEstimate(flops=10_000_000, bytes_accessed=1_000_000, transcendentals=0),
        compiler_params=pltpu.CompilerParams(vmem_limit_bytes=8 << 20),
        name="observers",
    )(harmonic_numbers, scale, observer_ids, observer_radius)
    pressure = pl.pallas_call(
        kernel,
        out_shape=jax.ShapeDtypeStruct((block_rows, harmonics, 2, LANES), jnp.float32),
        in_specs=[vmem] * 7,
        out_specs=vmem,
        scratch_shapes=[
            pltpu.VMEM((13, held, DEPTH, TILE), jnp.bfloat16),
            pltpu.VMEM((6, observers, LANES), jnp.float32),
            pltpu.VMEM((TILE // LANES * FEATURES * 8, LANES), jnp.float32),
            pltpu.VMEM((6, block_rows, LANES), jnp.float32),
        ],
        compiler_params=pltpu.CompilerParams(vmem_limit_bytes=32 << 20),
        name="panel_sum",
    )(table, got, scale, harm_rows, feat, hub, dense)
    return jnp.transpose(pressure, (0, 2, 1, 3))[None]


def solution(mesh):
    placed = (
        P("inst", None, ("panel", "obs")),
        P(None, ("panel", "obs")),
        P(("panel", "obs")),
        P(),
        P(),
        P("obs", None, None),
        P("obs", None, None),
    )
    return jax.shard_map(
        functools.partial(per_device, sizes=dict(mesh.shape)),
        mesh=mesh,
        in_specs=placed,
        out_specs=P("obs", ("inst", "panel"), None, None, None),
        check_vma=False,
    )
```
